32 devices in a mesh: node: 8 (over z, core), dev: 4 (over y, x).
Axes of the slice: x: 2, y: 2, z: 4, core: 2. Of those that a mesh axis runs over, the one named last changes fastest.
Arguments:
- blocks: bfloat16 [8, 4, 16, 7, 16, 256], P('node', 'dev'), may hold values from -6 to 6
- levels: int32 [8, 4, 16], P('node', 'dev'), may hold values from 0 to 3
- destinations: int32 [8, 4, 16], P('node', 'dev'), may hold values from 0 to 3, as said below
- speeds: float32 [7], replicated, may hold values from -1 to 1
- thresholds: float32 [7], replicated, may hold values from 0.1 to 1
Outputs:
- updated: bfloat16 [8, 4, 32, 7, 16, 256], P('node', 'dev')
- new_levels: int32 [8, 4, 32], P('node', 'dev')
The draws below stay inside these ranges and needn't reach their ends.
Inputs may be any that keep to these rules, and one draw needn't show every extreme that they name: `destinations`: at most 8 blocks of one device go to one device, and at most 32 blocks arrive at one device; in every group both bounds are reached.
All inputs are finite; a program needn't handle non-finite values.
Results may differ from the reference program's by a relative error of at most 0.001.
Values may be sent and summed in bfloat16 or wider, within the bound.
A program may use at most 64 MiB of HBM per device.

```python
import math
import jax
import jax.numpy as jnp
from jax import lax

QUANT = 7
EDGE = 16
LEVELS = 4
SLOTS = 16
GROUPS = 8
OWNERS = 4
NEW_CAP = 32


def draw_destinations(key, part):

    def one_group(group_key):
        rank_key, label_key, slot_key = jax.random.split(group_key, 3)
        sender_rank = jax.random.permutation(rank_key, OWNERS).astype(jnp.int32)
        labels = jax.random.permutation(label_key, OWNERS).astype(jnp.int32)
        slot_order = jax.vmap(lambda single_key: jax.random.permutation(single_key, SLOTS))(jax.random.split(slot_key, OWNERS)).astype(jnp.int32)
        serial = slot_order * OWNERS + sender_rank[:, None]
        others = 1 + jnp.mod(serial - 2 * SLOTS, OWNERS - 1)
        picked = jnp.where(serial < 2 * SLOTS, 0, others)
        return labels[picked].astype(jnp.int32)
    return jax.vmap(one_group)(jax.random.split(jax.random.fold_in(key, 17), GROUPS))


def place_ends(values, stream_key, smallest, high):
    longest = values.shape.index(max(values.shape))
    spots = []
    for shift in (0, 1):
        where = [jax.random.randint(jax.random.fold_in(stream_key, axis), (), 0, length) for axis, length in enumerate(values.shape)]
        where[longest] = (where[longest] + shift) % values.shape[longest]
        spots.append(tuple(where))
    return values.at[spots[0]].set(smallest).at[spots[1]].set(high)


def level_of(stream_key, extent, cuts, low, top_value):
    level = 1.0
    for dim, shards_of in cuts:
        heights = jax.random.uniform(jax.random.fold_in(jax.random.fold_in(stream_key, 6), dim), (shards_of,), jnp.float32, low / len(cuts), top_value / len(cuts))
        level = level * jnp.repeat(jnp.exp(heights), extent[dim] // shards_of).reshape((-1,) + (1,) * (len(extent) - 1 - dim))
    return level


def gaussian(stream_key, extent, scale, most, pieces=(), held_as=jnp.bfloat16):
    values = scale * jax.random.normal(stream_key, extent, jnp.float32)
    if pieces:
        values = values * level_of(stream_key, extent, pieces, -0.22, 0.18)
    return jnp.clip(values, -most, most).astype(held_as)


def setup_inputs(seed: int = 0) -> dict:
    splits = jax.random.split(jax.random.key(seed), 6)
    return {
        "blocks": gaussian(splits[0], (GROUPS, OWNERS, SLOTS, QUANT, EDGE, EDGE * EDGE), 1.0, 6.0, ((0, 8), (1, 4))),
        "levels": place_ends(jax.random.randint(splits[1], (GROUPS, OWNERS, SLOTS), 0, LEVELS), jax.random.fold_in(splits[1], 1), 0, LEVELS - 1).astype(jnp.int32),
        "destinations": draw_destinations(jax.random.fold_in(splits[5], 71), 0),
        "speeds": jnp.clip(jax.random.uniform(splits[3], (QUANT,), jnp.float32, -1.0, 1.0), -1.0, 1.0),
        "thresholds": jnp.clip(jnp.exp(jax.random.uniform(splits[4], (QUANT,), jnp.float32, math.log(0.1), math.log(1.0))), 0.1, 1.0),
    }


COURANT = 0.4
WENO_EPS = 1e-6


def square(value):
    return value * value


def weno_face(first, second, third, fourth, fifth):
    guess_zero = (2.0 * first - 7.0 * second + 11.0 * third) / 6.0
    guess_one = (-second + 5.0 * third + 2.0 * fourth) / 6.0
    guess_two = (2.0 * third + 5.0 * fourth - fifth) / 6.0
    smooth_zero = 13.0 / 12.0 * square(first - 2.0 * second + third) + 0.25 * square(first - 4.0 * second + 3.0 * third)
    smooth_one = 13.0 / 12.0 * square(second - 2.0 * third + fourth) + 0.25 * square(second - fourth)
    smooth_two = 13.0 / 12.0 * square(third - 2.0 * fourth + fifth) + 0.25 * square(3.0 * third - 4.0 * fourth + fifth)
    weight_zero = 0.1 / square(WENO_EPS + smooth_zero)
    weight_one = 0.6 / square(WENO_EPS + smooth_one)
    weight_two = 0.3 / square(WENO_EPS + smooth_two)
    total = weight_zero + weight_one + weight_two
    return (weight_zero * guess_zero + weight_one * guess_one + weight_two * guess_two) / total


def shape_ghosts(near_layers, near_tag, own_tag):
    same_level = near_layers[:, :, 0:3]
    finer_level = 0.5 * (near_layers[:, :, 0:6:2] + near_layers[:, :, 1:6:2])
    coarser = jnp.concatenate([near_layers[:, :, 0:1], near_layers[:, :, 0:1], near_layers[:, :, 1:2]], axis=2)
    offset = jnp.clip(near_tag - own_tag, -1, 1)[:, None, None, None]
    ghost_cells = jnp.where(offset > 0, finer_level, jnp.where(offset < 0, coarser, same_level))
    return lax.optimization_barrier(ghost_cells.astype(jnp.bfloat16))


def advance_quantity(extended, occupied, velocity, threshold):
    cells = extended.shape[1] - 6
    stencil = [extended[:, k:k + cells + 1] for k in range(6)]
    left_state = weno_face(stencil[0], stencil[1], stencil[2], stencil[3], stencil[4])
    right_state = weno_face(stencil[5], stencil[4], stencil[3], stencil[2], stencil[1])
    fluxes = jnp.maximum(velocity, 0.0) * left_state + jnp.minimum(velocity, 0.0) * right_state
    advanced = extended[:, 3:3 + cells] - COURANT * (fluxes[:, 1:] - fluxes[:, :-1])
    even_cells = advanced[:, 0::2]
    odd_cells = advanced[:, 1::2]
    predicted = jnp.concatenate([0.5 * (even_cells[:, :-1] + even_cells[:, 1:]), even_cells[:, -1:]], axis=1)
    detail = odd_cells - predicted
    kept_cells = predicted + detail - jnp.clip(detail, -threshold, threshold)
    result = jnp.stack([even_cells, kept_cells], axis=2).reshape(advanced.shape)
    return jnp.where(occupied[:, None, None], result, 0.0).astype(jnp.bfloat16)


def reference(blocks, levels, destinations, speeds, thresholds):
    flat_targets = destinations.reshape(GROUPS, OWNERS * SLOTS)
    owner_ids = jnp.arange(OWNERS).astype(jnp.int32)
    matches = (flat_targets[:, :, None] == owner_ids[None, None, :]).astype(jnp.int32)
    earlier = jnp.cumsum(matches, axis=1) - matches
    position = jnp.sum(earlier * matches, axis=2)
    target_index = (flat_targets * NEW_CAP + position).astype(jnp.int32)
    group_index = jnp.arange(GROUPS).astype(jnp.int32)[:, None]
    arranged = jnp.zeros((GROUPS, OWNERS * NEW_CAP, QUANT, EDGE, EDGE * EDGE), blocks.dtype)
    arranged = arranged.at[group_index, target_index].set(blocks.reshape(GROUPS, OWNERS * SLOTS, QUANT, EDGE, EDGE * EDGE))
    block_tag = jnp.zeros((GROUPS, OWNERS * NEW_CAP), jnp.int32)
    block_tag = block_tag.at[group_index, target_index].set((levels.reshape(GROUPS, OWNERS * SLOTS) + 1).astype(jnp.int32))
    below = arranged[:, :, :, EDGE - 6:]
    lower_faces = jnp.concatenate([jnp.zeros_like(below[:1]), below[:-1]], axis=0)
    above = arranged[:, :, :, :6]
    upper_faces = jnp.concatenate([above[1:], jnp.zeros_like(above[:1])], axis=0)
    lower_tags = jnp.concatenate([jnp.zeros_like(block_tag[:1]), block_tag[:-1]], axis=0)
    upper_tags = jnp.concatenate([block_tag[1:], jnp.zeros_like(block_tag[:1])], axis=0)

    def one_group(member):
        own_blocks, own_tag, lower_layers, lower_tag, upper_layers, upper_tag = member
        ghost_low = shape_ghosts(lower_layers.astype(jnp.float32)[:, :, ::-1], lower_tag, own_tag)[:, :, ::-1]
        ghost_high = shape_ghosts(upper_layers.astype(jnp.float32), upper_tag, own_tag)
        extended = jnp.concatenate([ghost_low, own_blocks, ghost_high], axis=2).astype(jnp.float32)
        extended = jnp.moveaxis(extended, 1, 0)
        occupied = own_tag > 0
        result = lax.map(lambda entry: advance_quantity(entry[0], occupied, entry[1], entry[2]), (extended, speeds, thresholds))
        return jnp.moveaxis(result, 0, 1)

    updated = lax.map(one_group, (arranged, block_tag, lower_faces, lower_tags, upper_faces, upper_tags))
    updated = updated.reshape(GROUPS, OWNERS, NEW_CAP, QUANT, EDGE, EDGE * EDGE)
    new_levels = (block_tag - 1).reshape(GROUPS, OWNERS, NEW_CAP)
    return updated, new_levels
```

```python
import functools

import jax
import jax.numpy as jnp
from jax import lax
from jax.experimental import pallas as pl
from jax.experimental.pallas import tpu as pltpu
from jax.sharding import PartitionSpec as P

NEW_CAP = 32
GHOST = 3
COURANT = 0.4
WENO_EPS = 1e-06
MESH = pl.DeviceIdType.MESH


def iota(shape, dim):
    return lax.broadcasted_iota(jnp.int32, shape, dim)


def split_low(values, size):
    return values & (size - 1)


def split_high(values, size):
    return values >> (size.bit_length() - 1)


def pack_kernel(owners, pair, dest_ref, level_ref, block_ref, out_ref, tags_ref, place_ref):
    slots, _, edge, plane = block_ref.shape
    rows = edge * pair
    lanes = slots * edge

    @pl.when(pl.program_id(0) == 0)
    def _():
        dest = [dest_ref[s] for s in range(slots)]
        within = []
        for s in range(slots):
            count = jnp.int32(0)
            for before in range(s):
                count = count + jnp.where(dest[before] == dest[s], 1, 0)
            within.append(count)
        lane = iota((1, lanes), 1)
        slot_of = split_high(lane, edge)
        target = jnp.zeros((1, lanes), jnp.int32)
        for s in range(slots):
            target = jnp.where(slot_of == s, dest[s] * rows + within[s], target)
        target = target + split_low(lane, edge) * pair
        hit = iota((owners * rows, lanes), 0) == target
        place_ref[...] = jnp.where(hit, 1.0, 0.0).astype(jnp.bfloat16)
        owner = iota(tags_ref.shape, 0)
        slot = split_low(iota(tags_ref.shape, 2), pair)
        tags = jnp.zeros(tags_ref.shape, jnp.int32)
        for s in range(slots):
            here = (owner == dest[s]) & (slot == within[s])
            tags = jnp.where(here, level_ref[s] + 1, tags)
        tags_ref[...] = tags

    payload = block_ref[...].reshape(lanes, plane)
    packed = jnp.dot(place_ref[...], payload, preferred_element_type=jnp.float32)
    out_ref[...] = packed.astype(jnp.bfloat16).reshape(owners, 1, rows, plane)


def advance_tile(cells, neg, speed, threshold):
    total = len(cells)
    edge = total - 2 * GHOST
    m = [jnp.where(neg, cells[total - 1 - i], cells[i]) for i in range(total)]
    d = [m[i + 1] - m[i] for i in range(total - 2)]
    d2 = [x + x for x in d]
    s = [None] + [d[i] - d[i - 1] for i in range(1, total - 2)]
    base = [None] + [(13.0 / 3.0) * (x * x) + 4.0 * WENO_EPS for x in s[1:]]
    shift = []
    for f in range(edge + 1):
        low, high = d[f + 1], d[f + 2]
        t0 = s[f + 1] + d2[f + 1]
        t1 = low + high
        t2 = d2[f + 2] - s[f + 3]
        b0 = base[f + 1] + t0 * t0
        b1 = base[f + 2] + t1 * t1
        b2 = base[f + 3] + t2 * t2
        w0, w1, w2 = b1 * b2, b0 * b2, b0 * b1
        w0, w1, w2 = w0 * w0, 6.0 * (w1 * w1), 3.0 * (w2 * w2)
        p0 = t0 + t0 - low
        p1 = low + d2[f + 2]
        p2 = t2 + high
        shift.append((w0 * p0 + w1 * p1 + w2 * p2) / (w0 + w1 + w2))
    full = COURANT * speed
    sixth = full / 6.0
    moved = [
        m[c + GHOST] - (full * d[c + 2] + sixth * (shift[c + 1] - shift[c]))
        for c in range(edge)
    ]
    adv = [jnp.where(neg, moved[edge - 1 - c], moved[c]) for c in range(edge)]
    result = list(adv)
    for k in range(1, edge, 2):
        guess = 0.5 * (adv[k - 1] + adv[k + 1]) if k + 1 < edge else adv[k - 1]
        detail = adv[k] - guess
        result[k] = guess + detail - jnp.clip(detail, -threshold, threshold)
    return result


def step_kernel(
    owners, groups, pair,
    packed_ref, tags_ref, speed_ref, threshold_ref,
    out_ref, levels_ref,
    inc, tin, unpack, ext, gsend, grecv, own_tag, near_tag, wide, obuf,
    tag_send, tag_recv, self_sem, blk_send, blk_recv,
    near_send, near_recv, gh_send, gh_recv, out_sem,
):
    node = lax.axis_index("node")
    me = lax.axis_index("dev")
    quant = inc.shape[0]
    rows, plane = inc.shape[2], inc.shape[3]
    edge = rows // pair
    cap = own_tag.shape[0]
    has_low = node > 0
    has_high = node < groups - 1

    barrier = pltpu.get_barrier_semaphore()
    for r in range(1, owners):
        pl.semaphore_signal(
            barrier, inc=1, device_id={"dev": lax.rem(me + r, owners)}, device_id_type=MESH
        )

    @pl.when(has_low)
    def _():
        pl.semaphore_signal(barrier, inc=1, device_id={"node": node - 1}, device_id_type=MESH)

    @pl.when(has_high)
    def _():
        pl.semaphore_signal(barrier, inc=1, device_id={"node": node + 1}, device_id_type=MESH)

    nears = (node + groups - 1) // groups + (2 * groups - 2 - node) // groups
    pl.semaphore_wait(barrier, owners - 1 + nears)

    def tag_copy(r):
        return pltpu.make_async_remote_copy(
            src_ref=tags_ref.at[lax.rem(me + r, owners)], dst_ref=tin.at[me],
            send_sem=tag_send.at[r], recv_sem=tag_recv.at[r],
            device_id={"dev": lax.rem(me + r, owners)}, device_id_type=MESH,
        )

    def tag_arrival(r):
        return pltpu.make_async_remote_copy(
            src_ref=tags_ref.at[me], dst_ref=tin.at[lax.rem(me + owners - r, owners)],
            send_sem=tag_send.at[r], recv_sem=tag_recv.at[r],
            device_id={"dev": lax.rem(me + r, owners)}, device_id_type=MESH,
        )

    def block_copy(q, r):
        to = lax.rem(me + r, owners)
        return pltpu.make_async_remote_copy(
            src_ref=packed_ref.at[to, q], dst_ref=inc.at[q, me],
            send_sem=blk_send.at[q, r], recv_sem=blk_recv.at[q, r],
            device_id={"dev": to}, device_id_type=MESH,
        )

    def block_arrival(q, r):
        return pltpu.make_async_remote_copy(
            src_ref=packed_ref.at[me, q], dst_ref=inc.at[q, lax.rem(me + owners - r, owners)],
            send_sem=blk_send.at[q, r], recv_sem=blk_recv.at[q, r],
            device_id={"dev": lax.rem(me + r, owners)}, device_id_type=MESH,
        )

    own_tags = pltpu.make_async_copy(tags_ref.at[me], tin.at[me], tag_send.at[0])

    def own_block(q):
        return pltpu.make_async_copy(packed_ref.at[me, q], inc.at[q, me], self_sem.at[q])

    own_tags.start()
    for r in range(1, owners):
        tag_copy(r).start()

    @pl.loop(0, quant)
    def _(q):
        own_block(q).start()
        for r in range(1, owners):
            block_copy(q, r).start()

    @pl.when(node == 0)
    def _():
        grecv[0] = jnp.zeros(grecv.shape[1:], grecv.dtype)
        near_tag[0] = jnp.zeros(near_tag.shape[1:], near_tag.dtype)

    @pl.when(node == groups - 1)
    def _():
        grecv[1] = jnp.zeros(grecv.shape[1:], grecv.dtype)
        near_tag[1] = jnp.zeros(near_tag.shape[1:], near_tag.dtype)

    own_tags.wait()
    for r in range(1, owners):
        tag_arrival(r).wait_recv()

    lane = iota((1, rows), 1)
    slot, cell = split_low(lane, pair), split_high(lane, pair)
    first = jnp.zeros((1, 1), jnp.float32)
    tag_sum = jnp.zeros((cap, rows), jnp.float32)
    row_p = iota((cap, rows), 0)
    targets = []
    for i in range(owners):
        tag = tin[i, 0:1, :]
        present = tag > 0
        position = first.astype(jnp.int32) + slot
        targets.append(jnp.where(present, cell * cap + position, -1))
        here = (row_p == jnp.where(present & (cell == 0), position, -1))
        tag_sum = tag_sum + jnp.where(here, tag.astype(jnp.float32), 0.0)
        count = jnp.sum(jnp.where(present, 1.0, 0.0), axis=1, keepdims=True)
        first = first + count * (1.0 / edge)
    tag_col = jnp.sum(tag_sum, axis=1, keepdims=True)
    tag_all = jnp.broadcast_to(tag_col, own_tag.shape)
    own_tag[...] = tag_all.astype(jnp.int32)
    levels_ref[...] = jnp.transpose(tag_all)[0:8, :].astype(jnp.int32) - 1
    row = iota((edge * cap, rows), 0)
    for i in range(owners):
        unpack[i] = jnp.where(row == targets[i], 1.0, 0.0).astype(jnp.bfloat16)

    def near_copy(up):
        to = node + 1 if up else node - 1
        index = 0 if up else 1
        return pltpu.make_async_remote_copy(
            src_ref=own_tag, dst_ref=near_tag.at[index],
            send_sem=near_send.at[index], recv_sem=near_recv.at[index],
            device_id={"node": to}, device_id_type=MESH,
        )

    def ghost_copy(q, up):
        to = node + 1 if up else node - 1
        index = 0 if up else 1
        return pltpu.make_async_remote_copy(
            src_ref=gsend.at[index, q], dst_ref=grecv.at[index, q],
            send_sem=gh_send.at[index, q], recv_sem=gh_recv.at[index, q],
            device_id={"node": to}, device_id_type=MESH,
        )

    @pl.when(has_high)
    def _():
        near_copy(True).start()

    @pl.when(has_low)
    def _():
        near_copy(False).start()

    @pl.when(has_low)
    def _():
        near_copy(True).wait_recv()

    @pl.when(has_high)
    def _():
        near_copy(False).wait_recv()

    def front(q):
        at = split_low(q, 2)
        own_block(q).wait()
        for r in range(1, owners):
            block_arrival(q, r).wait_recv()
        total = jnp.dot(unpack[0], inc[q, 0], preferred_element_type=jnp.float32)
        for i in range(1, owners):
            total = total + jnp.dot(unpack[i], inc[q, i], preferred_element_type=jnp.float32)
        ext[at, GHOST : GHOST + edge] = total.reshape(edge, cap, plane)
        for up in (True, False):
            index = 0 if up else 1
            gap = own_tag[...] - near_tag[1 - index]
            for half in range(plane // 128):
                lanes = slice(half * 128, half * 128 + 128)
                near = [
                    ext[at, GHOST + (edge - 1 - k if up else k), :, lanes]
                    for k in range(2 * GHOST)
                ]
                for k in range(GHOST):
                    finer = 0.5 * (near[2 * k] + near[2 * k + 1])
                    ghost = jnp.where(gap > 0, finer, jnp.where(gap < 0, near[k // 2 if k else 0], near[k]))
                    gsend[index, q, GHOST - 1 - k if up else k, :, lanes] = ghost.astype(jnp.bfloat16)

    def send(q):
        @pl.when(has_high)
        def _():
            ghost_copy(q, True).start()

        @pl.when(has_low)
        def _():
            ghost_copy(q, False).start()

    lane_tiles = plane // 128
    tiles = (cap // 8) * lane_tiles

    def tiles_of(q, start, stop):
        at = split_low(q, 2)
        speed, threshold = speed_ref[q], threshold_ref[q]
        neg = jnp.full((8, 128), speed, jnp.float32) < 0.0
        size = jnp.full((8, 128), jnp.abs(speed), jnp.float32)
        bound = jnp.full((8, 128), threshold, jnp.float32)

        def one(tile, carry):
            top = pl.multiple_of((tile // lane_tiles) * 8, 8)
            lanes = pl.ds(pl.multiple_of((tile % lane_tiles) * 128, 128), 128)
            cells = [ext[at, i, pl.ds(top, 8), lanes] for i in range(edge + 2 * GHOST)]
            result = advance_tile(cells, neg, size, bound)
            occupied = own_tag[pl.ds(top, 8), :] > 0
            for c in range(edge):
                value = jnp.where(occupied, result[c], 0.0)
                wide[tile % lane_tiles, pl.ds(top * edge + c, 8, stride=edge), :] = value
            return carry

        lax.fori_loop(start, stop, one, 0)

    def back_first(q):
        at = split_low(q, 2)

        @pl.when(has_low)
        def _():
            ghost_copy(q, True).wait_recv()

        @pl.when(has_high)
        def _():
            ghost_copy(q, False).wait_recv()

        ext[at, 0:GHOST] = grecv[0, q].astype(jnp.float32)
        ext[at, GHOST + edge :] = grecv[1, q].astype(jnp.float32)
        tiles_of(q, 0, tiles // 2)

    def out_copy(q):
        return pltpu.make_async_copy(obuf.at[q], out_ref.at[:, q], out_sem.at[q])

    def back_second(q):
        tiles_of(q, tiles // 2, tiles)
        for half in range(lane_tiles):
            obuf[q, :, :, half * 128 : half * 128 + 128] = (
                wide[half].astype(jnp.bfloat16).reshape(cap, edge, 128)
            )
        out_copy(q).start()

    front(jnp.int32(0))
    send(jnp.int32(0))

    @pl.loop(1, quant)
    def _(q):
        front(q)
        back_first(q - 1)
        send(q)
        back_second(q - 1)

    last = jnp.int32(quant - 1)
    back_first(last)
    back_second(last)

    for r in range(1, owners):
        tag_copy(r).wait_send()

    @pl.when(has_high)
    def _():
        near_copy(True).wait_send()

    @pl.when(has_low)
    def _():
        near_copy(False).wait_send()

    @pl.loop(0, quant)
    def _(q):
        for r in range(1, owners):
            block_copy(q, r).wait_send()

        @pl.when(has_high)
        def _():
            ghost_copy(q, True).wait_send()

        @pl.when(has_low)
        def _():
            ghost_copy(q, False).wait_send()

        out_copy(q).wait()


def body(blocks, levels, destinations, speeds, thresholds):
    owners, groups = lax.axis_size("dev"), lax.axis_size("node")
    _, _, slots, quant, edge, plane = blocks.shape
    pair = max(1, (2 * slots + owners - 1) // owners)
    rows = edge * pair
    smem = pl.BlockSpec(memory_space=pltpu.SMEM)
    anywhere = pl.BlockSpec(memory_space=pl.ANY)
    packed, tags = pl.pallas_call(
        functools.partial(pack_kernel, owners, pair),
        grid=(quant,),
        in_specs=[smem, smem, pl.BlockSpec((slots, 1, edge, plane), lambda q: (0, q, 0, 0))],
        out_specs=[
            pl.BlockSpec((owners, 1, rows, plane), lambda q: (0, q, 0, 0)),
            pl.BlockSpec((owners, 8, rows), lambda q: (0, 0, 0)),
        ],
        out_shape=[
            jax.ShapeDtypeStruct((owners, quant, rows, plane), jnp.bfloat16),
            jax.ShapeDtypeStruct((owners, 8, rows), jnp.int32),
        ],
        scratch_shapes=[pltpu.VMEM((owners * rows, slots * edge), jnp.bfloat16)],
        name="pack",
    )(destinations[0, 0], levels[0, 0], blocks[0, 0])

    cells = edge + 2 * GHOST
    dma = pltpu.SemaphoreType.DMA
    updated, new_levels = pl.pallas_call(
        functools.partial(step_kernel, owners, groups, pair),
        in_specs=[anywhere, anywhere, smem, smem],
        out_specs=[anywhere, pl.BlockSpec(memory_space=pltpu.VMEM)],
        out_shape=[
            jax.ShapeDtypeStruct((NEW_CAP, quant, edge, plane), jnp.bfloat16),
            jax.ShapeDtypeStruct((8, NEW_CAP), jnp.int32),
        ],
        scratch_shapes=[
            pltpu.VMEM((quant, owners, rows, plane), jnp.bfloat16),
            pltpu.VMEM((owners, 8, rows), jnp.int32),
            pltpu.VMEM((owners, edge * NEW_CAP, rows), jnp.bfloat16),
            pltpu.VMEM((2, cells, NEW_CAP, plane), jnp.float32),
            pltpu.VMEM((2, quant, GHOST, NEW_CAP, plane), jnp.bfloat16),
            pltpu.VMEM((2, quant, GHOST, NEW_CAP, plane), jnp.bfloat16),
            pltpu.VMEM((NEW_CAP, 128), jnp.int32),
            pltpu.VMEM((2, NEW_CAP, 128), jnp.int32),
            pltpu.VMEM((plane // 128, NEW_CAP * edge, 128), jnp.float32),
            pltpu.VMEM((quant, NEW_CAP, edge, plane), jnp.bfloat16),
            dma((owners,)), dma((owners,)), dma((quant,)),
            dma((quant, owners)), dma((quant, owners)),
            dma((2,)), dma((2,)), dma((2, quant)), dma((2, quant)), dma((quant,)),
        ],
        compiler_params=pltpu.CompilerParams(
            collective_id=0, has_side_effects=True, vmem_limit_bytes=48 * 1024 * 1024
        ),
        name="step",
    )(packed, tags, speeds, thresholds)
    return (
        updated.reshape(1, 1, NEW_CAP, quant, edge, plane),
        new_levels[0].reshape(1, 1, NEW_CAP),
    )


def solution(mesh):
    return jax.shard_map(
        body,
        mesh=mesh,
        in_specs=(
            P("node", "dev", None, None, None, None),
            P("node", "dev", None),
            P("node", "dev", None),
            P(),
            P(),
        ),
        out_specs=(P("node", "dev", None, None, None, None), P("node", "dev", None)),
        check_vma=False,
    )
```

```python
import functools

import jax
import jax.numpy as jnp
from jax import lax
from jax.experimental import pallas as pl
from jax.experimental.pallas import tpu as pltpu
from jax.sharding import PartitionSpec as P

NEW_CAP = 32
GHOST = 3
COURANT = 0.4
WENO_EPS = 1e-06
MESH = pl.DeviceIdType.MESH


def iota(shape, dim):
    return lax.broadcasted_iota(jnp.int32, shape, dim)


def split_low(values, size):
    return values & (size - 1)


def split_high(values, size):
    return values >> (size.bit_length() - 1)


def plan_sends(owners, pair, edge, dest_ref, level_ref, place_ref, tags_ref):
    slots = dest_ref.shape[0]
    rows = edge * pair
    lanes = slots * edge
    dest = [dest_ref[s] for s in range(slots)]
    within = []
    for s in range(slots):
        count = jnp.int32(0)
        for before in range(s):
            count = count + jnp.where(dest[before] == dest[s], 1, 0)
        within.append(count)
    lane = iota((1, lanes), 1)
    slot_of = split_high(lane, edge)
    target = jnp.zeros((1, lanes), jnp.int32)
    for s in range(slots):
        target = jnp.where(slot_of == s, dest[s] * rows + within[s], target)
    target = target + split_low(lane, edge) * pair
    hit = iota((owners * rows, lanes), 0) == target
    place_ref[...] = jnp.where(hit, 1.0, 0.0).astype(jnp.bfloat16)
    owner = iota(tags_ref.shape, 0)
    slot = split_low(iota(tags_ref.shape, 2), pair)
    tags = jnp.zeros(tags_ref.shape, jnp.int32)
    for s in range(slots):
        here = (owner == dest[s]) & (slot == within[s])
        tags = jnp.where(here, level_ref[s] + 1, tags)
    tags_ref[...] = tags


def advance_tile(cells, neg, speed, threshold):
    total = len(cells)
    edge = total - 2 * GHOST
    m = [jnp.where(neg, cells[total - 1 - i], cells[i]) for i in range(total)]
    d = [m[i + 1] - m[i] for i in range(total - 2)]
    d2 = [x + x for x in d]
    s = [None] + [d[i] - d[i - 1] for i in range(1, total - 2)]
    base = [None] + [(13.0 / 3.0) * (x * x) + 4.0 * WENO_EPS for x in s[1:]]
    shift = []
    for f in range(edge + 1):
        low, high = d[f + 1], d[f + 2]
        t0 = s[f + 1] + d2[f + 1]
        t1 = low + high
        t2 = d2[f + 2] - s[f + 3]
        b0 = base[f + 1] + t0 * t0
        b1 = base[f + 2] + t1 * t1
        b2 = base[f + 3] + t2 * t2
        w0, w1, w2 = b1 * b2, b0 * b2, b0 * b1
        w0, w1, w2 = w0 * w0, 6.0 * (w1 * w1), 3.0 * (w2 * w2)
        p0 = t0 + t0 - low
        p1 = low + d2[f + 2]
        p2 = t2 + high
        shift.append((w0 * p0 + w1 * p1 + w2 * p2) / (w0 + w1 + w2))
    full = COURANT * speed
    sixth = full / 6.0
    moved = [
        m[c + GHOST] - (full * d[c + 2] + sixth * (shift[c + 1] - shift[c]))
        for c in range(edge)
    ]
    adv = [jnp.where(neg, moved[edge - 1 - c], moved[c]) for c in range(edge)]
    result = list(adv)
    for k in range(1, edge, 2):
        guess = 0.5 * (adv[k - 1] + adv[k + 1]) if k + 1 < edge else adv[k - 1]
        detail = adv[k] - guess
        result[k] = guess + detail - jnp.clip(detail, -threshold, threshold)
    return result


def step_kernel(
    owners, groups, pair,
    dest_hbm, level_hbm, block_hbm, speed_hbm, threshold_hbm,
    out_ref, levels_ref,
    dest_ref, level_ref, speed_ref, threshold_ref,
    payload, place, packed_ref, tags_ref,
    inc, tin, unpack, ext, gsend, grecv, own_tag, near_tag, wide, obuf,
    load_sem, block_sem, tag_send, tag_recv, blk_send, blk_recv,
    near_send, near_recv, gh_send, gh_recv, out_sem,
):
    node = lax.axis_index("node")
    me = lax.axis_index("dev")
    slots, quant, edge, plane = block_hbm.shape
    rows = edge * pair
    cap = own_tag.shape[0]
    has_low = node > 0
    has_high = node < groups - 1

    small = [
        pltpu.make_async_copy(source, target, load_sem.at[n])
        for n, (source, target) in enumerate(
            (
                (dest_hbm, dest_ref), (level_hbm, level_ref),
                (speed_hbm, speed_ref), (threshold_hbm, threshold_ref),
            )
        )
    ]
    for copy in small:
        copy.start()

    def load(q):
        return pltpu.make_async_copy(block_hbm.at[:, q], payload.at[q], block_sem.at[q])

    @pl.loop(0, quant)
    def _(q):
        load(q).start()

    barrier = pltpu.get_barrier_semaphore()
    for r in range(1, owners):
        pl.semaphore_signal(
            barrier, inc=1, device_id={"dev": lax.rem(me + r, owners)}, device_id_type=MESH
        )

    @pl.when(has_low)
    def _():
        pl.semaphore_signal(barrier, inc=1, device_id={"node": node - 1}, device_id_type=MESH)

    @pl.when(has_high)
    def _():
        pl.semaphore_signal(barrier, inc=1, device_id={"node": node + 1}, device_id_type=MESH)

    for copy in small:
        copy.wait()
    plan_sends(owners, pair, edge, dest_ref, level_ref, place, tags_ref)
    nears = (node + groups - 1) // groups + (2 * groups - 2 - node) // groups
    pl.semaphore_wait(barrier, owners - 1 + nears)

    def tag_copy(r):
        return pltpu.make_async_remote_copy(
            src_ref=tags_ref.at[lax.rem(me + r, owners)], dst_ref=tin.at[me],
            send_sem=tag_send.at[r], recv_sem=tag_recv.at[r],
            device_id={"dev": lax.rem(me + r, owners)}, device_id_type=MESH,
        )

    def tag_arrival(r):
        return pltpu.make_async_remote_copy(
            src_ref=tags_ref.at[me], dst_ref=tin.at[lax.rem(me + owners - r, owners)],
            send_sem=tag_send.at[r], recv_sem=tag_recv.at[r],
            device_id={"dev": lax.rem(me + r, owners)}, device_id_type=MESH,
        )

    def block_copy(q, r):
        to = lax.rem(me + r, owners)
        return pltpu.make_async_remote_copy(
            src_ref=packed_ref.at[q, to], dst_ref=inc.at[q, me],
            send_sem=blk_send.at[q, r], recv_sem=blk_recv.at[q, r],
            device_id={"dev": to}, device_id_type=MESH,
        )

    def block_arrival(q, r):
        return pltpu.make_async_remote_copy(
            src_ref=packed_ref.at[q, me], dst_ref=inc.at[q, lax.rem(me + owners - r, owners)],
            send_sem=blk_send.at[q, r], recv_sem=blk_recv.at[q, r],
            device_id={"dev": lax.rem(me + r, owners)}, device_id_type=MESH,
        )

    def pack(q):
        load(q).wait()
        flat = payload[q].reshape(slots * edge, plane)
        rows_of = jnp.dot(place[...], flat, preferred_element_type=jnp.float32)
        packed_ref[q] = rows_of.astype(jnp.bfloat16).reshape(owners, rows, plane)

    def launch(q):
        for r in range(1, owners):
            block_copy(q, r).start()

    tin[me] = tags_ref[me]
    pack(jnp.int32(0))
    for r in range(1, owners):
        tag_copy(r).start()

    @pl.loop(1, quant)
    def _(q):
        pack(q)
        launch(q - 1)
        inc[q - 1, me] = packed_ref[q - 1, me]

    launch(jnp.int32(quant - 1))
    inc[quant - 1, me] = packed_ref[quant - 1, me]

    @pl.when(node == 0)
    def _():
        grecv[0] = jnp.zeros(grecv.shape[1:], grecv.dtype)
        near_tag[0] = jnp.zeros(near_tag.shape[1:], near_tag.dtype)

    @pl.when(node == groups - 1)
    def _():
        grecv[1] = jnp.zeros(grecv.shape[1:], grecv.dtype)
        near_tag[1] = jnp.zeros(near_tag.shape[1:], near_tag.dtype)

    for r in range(1, owners):
        tag_arrival(r).wait_recv()

    lane = iota((1, rows), 1)
    slot, cell = split_low(lane, pair), split_high(lane, pair)
    first = jnp.zeros((1, 1), jnp.float32)
    tag_sum = jnp.zeros((cap, rows), jnp.float32)
    row_p = iota((cap, rows), 0)
    targets = []
    for i in range(owners):
        tag = tin[i, 0:1, :]
        present = tag > 0
        position = first.astype(jnp.int32) + slot
        targets.append(jnp.where(present, cell * cap + position, -1))
        here = (row_p == jnp.where(present & (cell == 0), position, -1))
        tag_sum = tag_sum + jnp.where(here, tag.astype(jnp.float32), 0.0)
        count = jnp.sum(jnp.where(present, 1.0, 0.0), axis=1, keepdims=True)
        first = first + count * (1.0 / edge)
    tag_col = jnp.sum(tag_sum, axis=1, keepdims=True)
    tag_all = jnp.broadcast_to(tag_col, own_tag.shape)
    own_tag[...] = tag_all.astype(jnp.int32)
    levels_ref[...] = jnp.transpose(tag_all)[0:8, :].astype(jnp.int32) - 1
    row = iota((edge * cap, rows), 0)
    for i in range(owners):
        hit = jnp.where(row == targets[i], 1.0, 0.0).astype(jnp.bfloat16)
        unpack[:, i * rows : i * rows + rows] = hit

    def near_copy(up):
        to = node + 1 if up else node - 1
        index = 0 if up else 1
        return pltpu.make_async_remote_copy(
            src_ref=own_tag, dst_ref=near_tag.at[index],
            send_sem=near_send.at[index], recv_sem=near_recv.at[index],
            device_id={"node": to}, device_id_type=MESH,
        )

    def ghost_copy(q, up):
        to = node + 1 if up else node - 1
        index = 0 if up else 1
        return pltpu.make_async_remote_copy(
            src_ref=gsend.at[index, q], dst_ref=grecv.at[index, q],
            send_sem=gh_send.at[index, q], recv_sem=gh_recv.at[index, q],
            device_id={"node": to}, device_id_type=MESH,
        )

    @pl.when(has_high)
    def _():
        near_copy(True).start()

    @pl.when(has_low)
    def _():
        near_copy(False).start()

    @pl.when(has_low)
    def _():
        near_copy(True).wait_recv()

    @pl.when(has_high)
    def _():
        near_copy(False).wait_recv()

    def front(q):
        at = split_low(q, 2)
        for r in range(1, owners):
            block_arrival(q, r).wait_recv()
        total = jnp.dot(
            unpack[...], inc[q].reshape(owners * rows, plane), preferred_element_type=jnp.float32
        )
        ext[at, GHOST : GHOST + edge] = total.reshape(edge, cap, plane)
        for up in (True, False):
            index = 0 if up else 1
            gap = own_tag[...] - near_tag[1 - index]
            for half in range(plane // 128):
                lanes = slice(half * 128, half * 128 + 128)
                near = [
                    ext[at, GHOST + (edge - 1 - k if up else k), :, lanes]
                    for k in range(2 * GHOST)
                ]
                for k in range(GHOST):
                    finer = 0.5 * (near[2 * k] + near[2 * k + 1])
                    ghost = jnp.where(gap > 0, finer, jnp.where(gap < 0, near[k // 2 if k else 0], near[k]))
                    gsend[index, q, GHOST - 1 - k if up else k, :, lanes] = ghost.astype(jnp.bfloat16)

    def send(q):
        @pl.when(has_high)
        def _():
            ghost_copy(q, True).start()

        @pl.when(has_low)
        def _():
            ghost_copy(q, False).start()

    lane_tiles = plane // 128
    tiles = (cap // 8) * lane_tiles

    def tiles_of(q, start, stop):
        at = split_low(q, 2)
        speed, threshold = speed_ref[q], threshold_ref[q]
        neg = jnp.full((8, 128), speed, jnp.float32) < 0.0
        size = jnp.full((8, 128), jnp.abs(speed), jnp.float32)
        bound = jnp.full((8, 128), threshold, jnp.float32)

        def one(tile, carry):
            top = pl.multiple_of((tile // lane_tiles) * 8, 8)
            lanes = pl.ds(pl.multiple_of((tile % lane_tiles) * 128, 128), 128)
            cells = [ext[at, i, pl.ds(top, 8), lanes] for i in range(edge + 2 * GHOST)]
            result = advance_tile(cells, neg, size, bound)
            occupied = own_tag[pl.ds(top, 8), :] > 0
            for c in range(edge):
                value = jnp.where(occupied, result[c], 0.0)
                wide[tile % lane_tiles, pl.ds(top * edge + c, 8, stride=edge), :] = value
            return carry

        lax.fori_loop(start, stop, one, 0)

    def back_first(q):
        at = split_low(q, 2)

        @pl.when(has_low)
        def _():
            ghost_copy(q, True).wait_recv()

        @pl.when(has_high)
        def _():
            ghost_copy(q, False).wait_recv()

        ext[at, 0:GHOST] = grecv[0, q].astype(jnp.float32)
        ext[at, GHOST + edge :] = grecv[1, q].astype(jnp.float32)
        tiles_of(q, 0, tiles // 2)

    def out_copy(q):
        return pltpu.make_async_copy(obuf.at[q], out_ref.at[:, q], out_sem.at[q])

    def back_second(q):
        tiles_of(q, tiles // 2, tiles)
        for half in range(lane_tiles):
            obuf[q, :, :, half * 128 : half * 128 + 128] = (
                wide[half].astype(jnp.bfloat16).reshape(cap, edge, 128)
            )
        out_copy(q).start()

    front(jnp.int32(0))
    send(jnp.int32(0))

    @pl.loop(1, quant)
    def _(q):
        front(q)
        back_first(q - 1)
        send(q)
        back_second(q - 1)

    last = jnp.int32(quant - 1)
    back_first(last)
    back_second(last)

    for r in range(1, owners):
        tag_copy(r).wait_send()

    @pl.when(has_high)
    def _():
        near_copy(True).wait_send()

    @pl.when(has_low)
    def _():
        near_copy(False).wait_send()

    @pl.loop(0, quant)
    def _(q):
        for r in range(1, owners):
            block_copy(q, r).wait_send()

        @pl.when(has_high)
        def _():
            ghost_copy(q, True).wait_send()

        @pl.when(has_low)
        def _():
            ghost_copy(q, False).wait_send()

        out_copy(q).wait()


def body(blocks, levels, destinations, speeds, thresholds):
    owners, groups = lax.axis_size("dev"), lax.axis_size("node")
    _, _, slots, quant, edge, plane = blocks.shape
    pair = max(1, (2 * slots + owners - 1) // owners)
    rows = edge * pair
    cells = edge + 2 * GHOST
    dma = pltpu.SemaphoreType.DMA
    updated, new_levels = pl.pallas_call(
        functools.partial(step_kernel, owners, groups, pair),
        in_specs=[pl.BlockSpec(memory_space=pltpu.HBM)] * 5,
        out_specs=[
            pl.BlockSpec(memory_space=pltpu.HBM), pl.BlockSpec(memory_space=pltpu.VMEM)
        ],
        out_shape=[
            jax.ShapeDtypeStruct((NEW_CAP, quant, edge, plane), jnp.bfloat16),
            jax.ShapeDtypeStruct((8, NEW_CAP), jnp.int32),
        ],
        scratch_shapes=[
            pltpu.SMEM((slots,), jnp.int32), pltpu.SMEM((slots,), jnp.int32),
            pltpu.SMEM((quant,), jnp.float32), pltpu.SMEM((quant,), jnp.float32),
            pltpu.VMEM((quant, slots, edge, plane), jnp.bfloat16),
            pltpu.VMEM((owners * rows, slots * edge), jnp.bfloat16),
            pltpu.VMEM((quant, owners, rows, plane), jnp.bfloat16),
            pltpu.VMEM((owners, 8, rows), jnp.int32),
            pltpu.VMEM((quant, owners, rows, plane), jnp.bfloat16),
            pltpu.VMEM((owners, 8, rows), jnp.int32),
            pltpu.VMEM((edge * NEW_CAP, owners * rows), jnp.bfloat16),
            pltpu.VMEM((2, cells, NEW_CAP, plane), jnp.float32),
            pltpu.VMEM((2, quant, GHOST, NEW_CAP, plane), jnp.bfloat16),
            pltpu.VMEM((2, quant, GHOST, NEW_CAP, plane), jnp.bfloat16),
            pltpu.VMEM((NEW_CAP, 128), jnp.int32),
            pltpu.VMEM((2, NEW_CAP, 128), jnp.int32),
            pltpu.VMEM((plane // 128, NEW_CAP * edge, 128), jnp.float32),
            pltpu.VMEM((quant, NEW_CAP, edge, plane), jnp.bfloat16),
            dma((4,)), dma((quant,)), dma((owners,)), dma((owners,)),
            dma((quant, owners)), dma((quant, owners)),
            dma((2,)), dma((2,)), dma((2, quant)), dma((2, quant)), dma((quant,)),
        ],
        compiler_params=pltpu.CompilerParams(
            collective_id=0, has_side_effects=True, vmem_limit_bytes=67_000_000
        ),
        name="step",
    )(destinations[0, 0], levels[0, 0], blocks[0, 0], speeds, thresholds)
    return (
        updated.reshape(1, 1, NEW_CAP, quant, edge, plane),
        new_levels[0].reshape(1, 1, NEW_CAP),
    )


def solution(mesh):
    return jax.shard_map(
        body,
        mesh=mesh,
        in_specs=(
            P("node", "dev", None, None, None, None),
            P("node", "dev", None),
            P("node", "dev", None),
            P(),
            P(),
        ),
        out_specs=(P("node", "dev", None, None, None, None), P("node", "dev", None)),
        check_vma=False,
    )
```

```python
import functools

import jax
import jax.numpy as jnp
from jax import lax
from jax.experimental import pallas as pl
from jax.experimental.pallas import tpu as pltpu
from jax.sharding import PartitionSpec as P

NEW_CAP = 32
GHOST = 3
COURANT = 0.4
WENO_EPS = 1e-06
MESH = pl.DeviceIdType.MESH


def iota(shape, dim):
    return lax.broadcasted_iota(jnp.int32, shape, dim)


def split_low(values, size):
    return values & (size - 1)


def partner(me, r):
    result, bit = 0, 1
    while bit <= r:
        own = me // bit % 2
        result = result + bit * ((1 - own) if r & bit else own)
        bit *= 2
    return result + me // bit * bit


def split_high(values, size):
    return values >> (size.bit_length() - 1)


def plan_sends(owners, pair, edge, dest_ref, level_ref, place_ref, tags_ref):
    slots = dest_ref.shape[0]
    rows = edge * pair
    lanes = slots * edge
    dest = [dest_ref[s] for s in range(slots)]
    within = []
    for s in range(slots):
        count = jnp.int32(0)
        for before in range(s):
            count = count + jnp.where(dest[before] == dest[s], 1, 0)
        within.append(count)
    lane = iota((1, lanes), 1)
    slot_of = split_high(lane, edge)
    target = jnp.zeros((1, lanes), jnp.int32)
    for s in range(slots):
        target = jnp.where(slot_of == s, dest[s] * rows + within[s], target)
    target = target + split_low(lane, edge) * pair
    hit = iota((owners * rows, lanes), 0) == target
    place_ref[...] = jnp.where(hit, 1.0, 0.0).astype(jnp.bfloat16)
    owner = iota(tags_ref.shape, 0)
    slot = split_low(iota(tags_ref.shape, 2), pair)
    tags = jnp.zeros(tags_ref.shape, jnp.int32)
    for s in range(slots):
        here = (owner == dest[s]) & (slot == within[s])
        tags = jnp.where(here, level_ref[s] + 1, tags)
    tags_ref[...] = tags


def advance_tile(cells, neg, speed, threshold):
    total = len(cells)
    edge = total - 2 * GHOST
    m = [jnp.where(neg, cells[total - 1 - i], cells[i]) for i in range(total)]
    d = [m[i + 1] - m[i] for i in range(total - 2)]
    d2 = [x + x for x in d]
    s = [None] + [d[i] - d[i - 1] for i in range(1, total - 2)]
    base = [None] + [(13.0 / 3.0) * (x * x) + 4.0 * WENO_EPS for x in s[1:]]
    shift = []
    for f in range(edge + 1):
        low, high = d[f + 1], d[f + 2]
        t0 = s[f + 1] + d2[f + 1]
        t1 = low + high
        t2 = d2[f + 2] - s[f + 3]
        b0 = base[f + 1] + t0 * t0
        b1 = base[f + 2] + t1 * t1
        b2 = base[f + 3] + t2 * t2
        w0, w1, w2 = b1 * b2, b0 * b2, b0 * b1
        w0, w1, w2 = w0 * w0, 6.0 * (w1 * w1), 3.0 * (w2 * w2)
        p0 = t0 + t0 - low
        p1 = low + d2[f + 2]
        p2 = t2 + high
        shift.append((w0 * p0 + w1 * p1 + w2 * p2) / (w0 + w1 + w2))
    full = COURANT * speed
    sixth = full / 6.0
    moved = [
        m[c + GHOST] - (full * d[c + 2] + sixth * (shift[c + 1] - shift[c]))
        for c in range(edge)
    ]
    adv = [jnp.where(neg, moved[edge - 1 - c], moved[c]) for c in range(edge)]
    result = list(adv)
    for k in range(1, edge, 2):
        guess = 0.5 * (adv[k - 1] + adv[k + 1]) if k + 1 < edge else adv[k - 1]
        detail = adv[k] - guess
        result[k] = guess + detail - jnp.clip(detail, -threshold, threshold)
    return result


def step_kernel(
    owners, groups, pair,
    dest_hbm, level_hbm, block_hbm, speed_hbm, threshold_hbm,
    out_ref, levels_ref,
    dest_ref, level_ref, speed_ref, threshold_ref,
    payload, place, packed_ref, tags_ref,
    inc, tin, unpack, ext, gsend, grecv, own_tag, near_tag, wide, obuf,
    load_sem, block_sem, tag_send, tag_recv, blk_send, blk_recv,
    near_send, near_recv, gh_send, gh_recv, out_sem,
):
    node = lax.axis_index("node")
    me = lax.axis_index("dev")
    slots, quant, edge, plane = block_hbm.shape
    rows = edge * pair
    cap = own_tag.shape[0]
    has_low = node > 0
    has_high = node < groups - 1

    small = [
        pltpu.make_async_copy(source, target, load_sem.at[n])
        for n, (source, target) in enumerate(
            (
                (dest_hbm, dest_ref), (level_hbm, level_ref),
                (speed_hbm, speed_ref), (threshold_hbm, threshold_ref),
            )
        )
    ]
    for copy in small:
        copy.start()

    def load(q):
        return pltpu.make_async_copy(block_hbm.at[:, q], payload.at[q], block_sem.at[q])

    @pl.loop(0, quant)
    def _(q):
        load(q).start()

    barrier = pltpu.get_barrier_semaphore()
    for r in range(1, owners):
        pl.semaphore_signal(
            barrier, inc=1, device_id={"dev": partner(me, r)}, device_id_type=MESH
        )

    @pl.when(has_low)
    def _():
        pl.semaphore_signal(barrier, inc=1, device_id={"node": node - 1}, device_id_type=MESH)

    @pl.when(has_high)
    def _():
        pl.semaphore_signal(barrier, inc=1, device_id={"node": node + 1}, device_id_type=MESH)

    for copy in small:
        copy.wait()
    plan_sends(owners, pair, edge, dest_ref, level_ref, place, tags_ref)
    nears = (node + groups - 1) // groups + (2 * groups - 2 - node) // groups
    pl.semaphore_wait(barrier, owners - 1 + nears)

    def tag_copy(r):
        return pltpu.make_async_remote_copy(
            src_ref=tags_ref.at[partner(me, r)], dst_ref=tin.at[me],
            send_sem=tag_send.at[r], recv_sem=tag_recv.at[r],
            device_id={"dev": partner(me, r)}, device_id_type=MESH,
        )

    def tag_arrival(r):
        return pltpu.make_async_remote_copy(
            src_ref=tags_ref.at[me], dst_ref=tin.at[partner(me, r)],
            send_sem=tag_send.at[r], recv_sem=tag_recv.at[r],
            device_id={"dev": partner(me, r)}, device_id_type=MESH,
        )

    def block_copy(q, r):
        to = partner(me, r)
        return pltpu.make_async_remote_copy(
            src_ref=packed_ref.at[q, to], dst_ref=inc.at[q, me],
            send_sem=blk_send.at[q, r], recv_sem=blk_recv.at[q, r],
            device_id={"dev": to}, device_id_type=MESH,
        )

    def block_arrival(q, r):
        return pltpu.make_async_remote_copy(
            src_ref=packed_ref.at[q, me], dst_ref=inc.at[q, partner(me, r)],
            send_sem=blk_send.at[q, r], recv_sem=blk_recv.at[q, r],
            device_id={"dev": partner(me, r)}, device_id_type=MESH,
        )

    def pack(q):
        load(q).wait()
        flat = payload[q].reshape(slots * edge, plane)
        rows_of = jnp.dot(place[...], flat, preferred_element_type=jnp.float32)
        packed_ref[q] = rows_of.astype(jnp.bfloat16).reshape(owners, rows, plane)

    def launch(q):
        for r in range(1, owners):
            block_copy(q, r).start()

    tin[me] = tags_ref[me]
    pack(jnp.int32(0))
    for r in range(1, owners):
        tag_copy(r).start()

    @pl.loop(1, quant)
    def _(q):
        pack(q)
        launch(q - 1)
        inc[q - 1, me] = packed_ref[q - 1, me]

    launch(jnp.int32(quant - 1))
    inc[quant - 1, me] = packed_ref[quant - 1, me]

    @pl.when(node == 0)
    def _():
        grecv[0] = jnp.zeros(grecv.shape[1:], grecv.dtype)
        near_tag[0] = jnp.zeros(near_tag.shape[1:], near_tag.dtype)

    @pl.when(node == groups - 1)
    def _():
        grecv[1] = jnp.zeros(grecv.shape[1:], grecv.dtype)
        near_tag[1] = jnp.zeros(near_tag.shape[1:], near_tag.dtype)

    for r in range(1, owners):
        tag_arrival(r).wait_recv()

    lane = iota((1, rows), 1)
    slot, cell = split_low(lane, pair), split_high(lane, pair)
    first = jnp.zeros((1, 1), jnp.float32)
    tag_sum = jnp.zeros((cap, rows), jnp.float32)
    row_p = iota((cap, rows), 0)
    targets = []
    for i in range(owners):
        tag = tin[i, 0:1, :]
        present = tag > 0
        position = first.astype(jnp.int32) + slot
        targets.append(jnp.where(present, cell * cap + position, -1))
        here = (row_p == jnp.where(present & (cell == 0), position, -1))
        tag_sum = tag_sum + jnp.where(here, tag.astype(jnp.float32), 0.0)
        count = jnp.sum(jnp.where(present, 1.0, 0.0), axis=1, keepdims=True)
        first = first + count * (1.0 / edge)
    tag_col = jnp.sum(tag_sum, axis=1, keepdims=True)
    tag_all = jnp.broadcast_to(tag_col, own_tag.shape)
    own_tag[...] = tag_all.astype(jnp.int32)
    levels_ref[...] = jnp.transpose(tag_all)[0:8, :].astype(jnp.int32) - 1
    row = iota((edge * cap, rows), 0)
    for i in range(owners):
        hit = jnp.where(row == targets[i], 1.0, 0.0).astype(jnp.bfloat16)
        unpack[:, i * rows : i * rows + rows] = hit

    def near_copy(up):
        to = node + 1 if up else node - 1
        index = 0 if up else 1
        return pltpu.make_async_remote_copy(
            src_ref=own_tag, dst_ref=near_tag.at[index],
            send_sem=near_send.at[index], recv_sem=near_recv.at[index],
            device_id={"node": to}, device_id_type=MESH,
        )

    def ghost_copy(q, up):
        to = node + 1 if up else node - 1
        index = 0 if up else 1
        return pltpu.make_async_remote_copy(
            src_ref=gsend.at[index, q], dst_ref=grecv.at[index, q],
            send_sem=gh_send.at[index, q], recv_sem=gh_recv.at[index, q],
            device_id={"node": to}, device_id_type=MESH,
        )

    @pl.when(has_high)
    def _():
        near_copy(True).start()

    @pl.when(has_low)
    def _():
        near_copy(False).start()

    @pl.when(has_low)
    def _():
        near_copy(True).wait_recv()

    @pl.when(has_high)
    def _():
        near_copy(False).wait_recv()

    def front(q):
        at = split_low(q, 2)
        for r in range(1, owners):
            block_arrival(q, r).wait_recv()
        sources = inc[q].reshape(owners * rows, plane)

        def arrange(low, high):
            part = jnp.dot(
                unpack[low * cap : high * cap, :], sources, preferred_element_type=jnp.float32
            )
            ext[at, GHOST + low : GHOST + high] = part.reshape(high - low, cap, plane)

        arrange(0, 2 * GHOST)
        arrange(edge - 2 * GHOST, edge)
        for up in (True, False):
            index = 0 if up else 1
            gap = own_tag[...] - near_tag[1 - index]
            for half in range(plane // 128):
                lanes = slice(half * 128, half * 128 + 128)
                near = [
                    ext[at, GHOST + (edge - 1 - k if up else k), :, lanes]
                    for k in range(2 * GHOST)
                ]
                for k in range(GHOST):
                    finer = 0.5 * (near[2 * k] + near[2 * k + 1])
                    ghost = jnp.where(gap > 0, finer, jnp.where(gap < 0, near[k // 2 if k else 0], near[k]))
                    gsend[index, q, GHOST - 1 - k if up else k, :, lanes] = ghost.astype(jnp.bfloat16)
        arrange(2 * GHOST, edge - 2 * GHOST)

    def send(q):
        @pl.when(has_high)
        def _():
            ghost_copy(q, True).start()

        @pl.when(has_low)
        def _():
            ghost_copy(q, False).start()

    lane_tiles = plane // 128
    tiles = (cap // 8) * lane_tiles

    def tiles_of(q):
        at = split_low(q, 2)
        speed, threshold = speed_ref[q], threshold_ref[q]
        neg = jnp.full((8, 128), speed, jnp.float32) < 0.0
        size = jnp.full((8, 128), jnp.abs(speed), jnp.float32)
        bound = jnp.full((8, 128), threshold, jnp.float32)

        def one(tile, carry):
            top = pl.multiple_of((tile // lane_tiles) * 8, 8)
            lanes = pl.ds(pl.multiple_of((tile % lane_tiles) * 128, 128), 128)
            cells = [ext[at, i, pl.ds(top, 8), lanes] for i in range(edge + 2 * GHOST)]
            result = advance_tile(cells, neg, size, bound)
            occupied = own_tag[pl.ds(top, 8), :] > 0
            for c in range(edge):
                value = jnp.where(occupied, result[c], 0.0)
                wide[tile % lane_tiles, pl.ds(top * edge + c, 8, stride=edge), :] = value
            return carry

        lax.fori_loop(0, tiles, one, 0)

    def out_copy(q):
        return pltpu.make_async_copy(obuf.at[q], out_ref.at[:, q], out_sem.at[q])

    def back(q):
        at = split_low(q, 2)

        @pl.when(has_low)
        def _():
            ghost_copy(q, True).wait_recv()

        @pl.when(has_high)
        def _():
            ghost_copy(q, False).wait_recv()

        ext[at, 0:GHOST] = grecv[0, q].astype(jnp.float32)
        ext[at, GHOST + edge :] = grecv[1, q].astype(jnp.float32)
        tiles_of(q)
        for half in range(lane_tiles):
            obuf[q, :, :, half * 128 : half * 128 + 128] = (
                wide[half].astype(jnp.bfloat16).reshape(cap, edge, 128)
            )
        out_copy(q).start()

    front(jnp.int32(0))
    send(jnp.int32(0))

    @pl.loop(1, quant)
    def _(q):
        front(q)
        send(q)
        back(q - 1)

    last = jnp.int32(quant - 1)
    back(last)

    for r in range(1, owners):
        tag_copy(r).wait_send()

    @pl.when(has_high)
    def _():
        near_copy(True).wait_send()

    @pl.when(has_low)
    def _():
        near_copy(False).wait_send()

    @pl.loop(0, quant)
    def _(q):
        for r in range(1, owners):
            block_copy(q, r).wait_send()

        @pl.when(has_high)
        def _():
            ghost_copy(q, True).wait_send()

        @pl.when(has_low)
        def _():
            ghost_copy(q, False).wait_send()

        out_copy(q).wait()


def body(blocks, levels, destinations, speeds, thresholds):
    owners, groups = lax.axis_size("dev"), lax.axis_size("node")
    _, _, slots, quant, edge, plane = blocks.shape
    pair = max(1, (2 * slots + owners - 1) // owners)
    rows = edge * pair
    cells = edge + 2 * GHOST
    dma = pltpu.SemaphoreType.DMA
    updated, new_levels = pl.pallas_call(
        functools.partial(step_kernel, owners, groups, pair),
        in_specs=[pl.BlockSpec(memory_space=pltpu.HBM)] * 5,
        out_specs=[
            pl.BlockSpec(memory_space=pltpu.HBM), pl.BlockSpec(memory_space=pltpu.VMEM)
        ],
        out_shape=[
            jax.ShapeDtypeStruct((NEW_CAP, quant, edge, plane), jnp.bfloat16),
            jax.ShapeDtypeStruct((8, NEW_CAP), jnp.int32),
        ],
        scratch_shapes=[
            pltpu.SMEM((slots,), jnp.int32), pltpu.SMEM((slots,), jnp.int32),
            pltpu.SMEM((quant,), jnp.float32), pltpu.SMEM((quant,), jnp.float32),
            pltpu.VMEM((quant, slots, edge, plane), jnp.bfloat16),
            pltpu.VMEM((owners * rows, slots * edge), jnp.bfloat16),
            pltpu.VMEM((quant, owners, rows, plane), jnp.bfloat16),
            pltpu.VMEM((owners, 8, rows), jnp.int32),
            pltpu.VMEM((quant, owners, rows, plane), jnp.bfloat16),
            pltpu.VMEM((owners, 8, rows), jnp.int32),
            pltpu.VMEM((edge * NEW_CAP, owners * rows), jnp.bfloat16),
            pltpu.VMEM((2, cells, NEW_CAP, plane), jnp.float32),
            pltpu.VMEM((2, quant, GHOST, NEW_CAP, plane), jnp.bfloat16),
            pltpu.VMEM((2, quant, GHOST, NEW_CAP, plane), jnp.bfloat16),
            pltpu.VMEM((NEW_CAP, 128), jnp.int32),
            pltpu.VMEM((2, NEW_CAP, 128), jnp.int32),
            pltpu.VMEM((plane // 128, NEW_CAP * edge, 128), jnp.float32),
            pltpu.VMEM((quant, NEW_CAP, edge, plane), jnp.bfloat16),
            dma((4,)), dma((quant,)), dma((owners,)), dma((owners,)),
            dma((quant, owners)), dma((quant, owners)),
            dma((2,)), dma((2,)), dma((2, quant)), dma((2, quant)), dma((quant,)),
        ],
        compiler_params=pltpu.CompilerParams(
            collective_id=0, has_side_effects=True, vmem_limit_bytes=67_000_000
        ),
        name="step",
    )(destinations[0, 0], levels[0, 0], blocks[0, 0], speeds, thresholds)
    return (
        updated.reshape(1, 1, NEW_CAP, quant, edge, plane),
        new_levels[0].reshape(1, 1, NEW_CAP),
    )


def solution(mesh):
    return jax.shard_map(
        body,
        mesh=mesh,
        in_specs=(
            P("node", "dev", None, None, None, None),
            P("node", "dev", None),
            P("node", "dev", None),
            P(),
            P(),
        ),
        out_specs=(P("node", "dev", None, None, None, None), P("node", "dev", None)),
        check_vma=False,
    )
```

```python
import functools

import jax
import jax.numpy as jnp
from jax import lax
from jax.experimental import pallas as pl
from jax.experimental.pallas import tpu as pltpu
from jax.sharding import PartitionSpec as P

NEW_CAP = 32
GHOST = 3
COURANT = 0.4
WENO_EPS = 1e-06
MESH = pl.DeviceIdType.MESH


def iota(shape, dim):
    return lax.broadcasted_iota(jnp.int32, shape, dim)


def split_low(values, size):
    return values & (size - 1)


def partner(me, r):
    result, bit = 0, 1
    while bit <= r:
        own = me // bit % 2
        result = result + bit * ((1 - own) if r & bit else own)
        bit *= 2
    return result + me // bit * bit


def split_high(values, size):
    return values >> (size.bit_length() - 1)


def plan_sends(owners, pair, edge, dest_ref, level_ref, place_ref, tags_ref):
    slots = dest_ref.shape[0]
    rows = edge * pair
    lanes = slots * edge
    dest = [dest_ref[s] for s in range(slots)]
    within = []
    for s in range(slots):
        count = jnp.int32(0)
        for before in range(s):
            count = count + jnp.where(dest[before] == dest[s], 1, 0)
        within.append(count)
    lane = iota((1, lanes), 1)
    slot_of = split_high(lane, edge)
    target = jnp.zeros((1, lanes), jnp.int32)
    for s in range(slots):
        target = jnp.where(slot_of == s, dest[s] * rows + within[s], target)
    target = target + split_low(lane, edge) * pair
    hit = iota((owners * rows, lanes), 0) == target
    place_ref[...] = jnp.where(hit, 1.0, 0.0).astype(jnp.bfloat16)
    owner = iota(tags_ref.shape, 0)
    slot = split_low(iota(tags_ref.shape, 2), pair)
    tags = jnp.zeros(tags_ref.shape, jnp.int32)
    for s in range(slots):
        here = (owner == dest[s]) & (slot == within[s])
        tags = jnp.where(here, level_ref[s] + 1, tags)
    tags_ref[...] = tags


def advance_tile(cells, neg, speed, threshold):
    total = len(cells)
    edge = total - 2 * GHOST
    m = [jnp.where(neg, cells[total - 1 - i], cells[i]) for i in range(total)]
    d = [m[i + 1] - m[i] for i in range(total - 2)]
    d2 = [x + x for x in d]
    s = [None] + [d[i] - d[i - 1] for i in range(1, total - 2)]
    base = [None] + [(13.0 / 3.0) * (x * x) + 4.0 * WENO_EPS for x in s[1:]]
    shift = []
    for f in range(edge + 1):
        low, high = d[f + 1], d[f + 2]
        t0 = s[f + 1] + d2[f + 1]
        t1 = low + high
        t2 = d2[f + 2] - s[f + 3]
        b0 = base[f + 1] + t0 * t0
        b1 = base[f + 2] + t1 * t1
        b2 = base[f + 3] + t2 * t2
        w0, w1, w2 = b1 * b2, b0 * b2, b0 * b1
        w0, w1, w2 = w0 * w0, 6.0 * (w1 * w1), 3.0 * (w2 * w2)
        p0 = t0 + t0 - low
        p1 = low + d2[f + 2]
        p2 = t2 + high
        shift.append((w0 * p0 + w1 * p1 + w2 * p2) / (w0 + w1 + w2))
    full = COURANT * speed
    sixth = full / 6.0
    moved = [
        m[c + GHOST] - (full * d[c + 2] + sixth * (shift[c + 1] - shift[c]))
        for c in range(edge)
    ]
    adv = [jnp.where(neg, moved[edge - 1 - c], moved[c]) for c in range(edge)]
    result = list(adv)
    for k in range(1, edge, 2):
        guess = 0.5 * (adv[k - 1] + adv[k + 1]) if k + 1 < edge else adv[k - 1]
        detail = adv[k] - guess
        result[k] = guess + detail - jnp.clip(detail, -threshold, threshold)
    return result


def step_kernel(
    owners, groups, pair,
    dest_hbm, level_hbm, block_hbm, speed_hbm, threshold_hbm,
    out_ref, levels_ref,
    dest_ref, level_ref, speed_ref, threshold_ref,
    payload, place, packed_ref, tags_ref,
    inc, tin, unpack, ext, gsend, grecv, own_tag, near_tag, wide,
    load_sem, block_sem, tag_send, tag_recv, blk_send, blk_recv,
    near_send, near_recv, gh_send, gh_recv,
):
    node = lax.axis_index("node")
    me = lax.axis_index("dev")
    slots, quant, edge, plane = block_hbm.shape
    rows = edge * pair
    cap = own_tag.shape[0]
    has_low = node > 0
    has_high = node < groups - 1

    small = [
        pltpu.make_async_copy(source, target, load_sem.at[n])
        for n, (source, target) in enumerate(
            (
                (dest_hbm, dest_ref), (level_hbm, level_ref),
                (speed_hbm, speed_ref), (threshold_hbm, threshold_ref),
            )
        )
    ]
    for copy in small:
        copy.start()

    def load(q):
        return pltpu.make_async_copy(block_hbm.at[:, q], payload.at[q], block_sem.at[q])

    @pl.loop(0, quant)
    def _(q):
        load(q).start()

    barrier = pltpu.get_barrier_semaphore()
    for r in range(1, owners):
        pl.semaphore_signal(
            barrier, inc=1, device_id={"dev": partner(me, r)}, device_id_type=MESH
        )

    @pl.when(has_low)
    def _():
        pl.semaphore_signal(barrier, inc=1, device_id={"node": node - 1}, device_id_type=MESH)

    @pl.when(has_high)
    def _():
        pl.semaphore_signal(barrier, inc=1, device_id={"node": node + 1}, device_id_type=MESH)

    for copy in small:
        copy.wait()
    plan_sends(owners, pair, edge, dest_ref, level_ref, place, tags_ref)
    nears = (node + groups - 1) // groups + (2 * groups - 2 - node) // groups
    pl.semaphore_wait(barrier, owners - 1 + nears)

    def tag_copy(r):
        return pltpu.make_async_remote_copy(
            src_ref=tags_ref.at[partner(me, r)], dst_ref=tin.at[me],
            send_sem=tag_send.at[r], recv_sem=tag_recv.at[r],
            device_id={"dev": partner(me, r)}, device_id_type=MESH,
        )

    def tag_arrival(r):
        return pltpu.make_async_remote_copy(
            src_ref=tags_ref.at[me], dst_ref=tin.at[partner(me, r)],
            send_sem=tag_send.at[r], recv_sem=tag_recv.at[r],
            device_id={"dev": partner(me, r)}, device_id_type=MESH,
        )

    def block_copy(q, r):
        to = partner(me, r)
        return pltpu.make_async_remote_copy(
            src_ref=packed_ref.at[q, to], dst_ref=inc.at[q, me],
            send_sem=blk_send.at[q, r], recv_sem=blk_recv.at[q, r],
            device_id={"dev": to}, device_id_type=MESH,
        )

    def block_arrival(q, r):
        return pltpu.make_async_remote_copy(
            src_ref=packed_ref.at[q, me], dst_ref=inc.at[q, partner(me, r)],
            send_sem=blk_send.at[q, r], recv_sem=blk_recv.at[q, r],
            device_id={"dev": partner(me, r)}, device_id_type=MESH,
        )

    def pack(q):
        load(q).wait()
        flat = payload[q].reshape(slots * edge, plane)
        rows_of = jnp.dot(place[...], flat, preferred_element_type=jnp.float32)
        packed_ref[q] = rows_of.astype(jnp.bfloat16).reshape(owners, rows, plane)

    def launch(q):
        for r in range(1, owners):
            block_copy(q, r).start()

    tin[me] = tags_ref[me]
    pack(jnp.int32(0))
    for r in range(1, owners):
        tag_copy(r).start()

    @pl.loop(1, quant)
    def _(q):
        pack(q)
        launch(q - 1)
        inc[q - 1, me] = packed_ref[q - 1, me]

    launch(jnp.int32(quant - 1))
    inc[quant - 1, me] = packed_ref[quant - 1, me]

    @pl.when(node == 0)
    def _():
        grecv[0] = jnp.zeros(grecv.shape[1:], grecv.dtype)
        near_tag[0] = jnp.zeros(near_tag.shape[1:], near_tag.dtype)

    @pl.when(node == groups - 1)
    def _():
        grecv[1] = jnp.zeros(grecv.shape[1:], grecv.dtype)
        near_tag[1] = jnp.zeros(near_tag.shape[1:], near_tag.dtype)

    for r in range(1, owners):
        tag_arrival(r).wait_recv()

    lane = iota((1, rows), 1)
    slot, cell = split_low(lane, pair), split_high(lane, pair)
    first = jnp.zeros((1, 1), jnp.float32)
    tag_sum = jnp.zeros((cap, rows), jnp.float32)
    row_p = iota((cap, rows), 0)
    targets = []
    for i in range(owners):
        tag = tin[i, 0:1, :]
        present = tag > 0
        position = first.astype(jnp.int32) + slot
        targets.append(jnp.where(present, cell * cap + position, -1))
        here = (row_p == jnp.where(present & (cell == 0), position, -1))
        tag_sum = tag_sum + jnp.where(here, tag.astype(jnp.float32), 0.0)
        count = jnp.sum(jnp.where(present, 1.0, 0.0), axis=1, keepdims=True)
        first = first + count * (1.0 / edge)
    tag_col = jnp.sum(tag_sum, axis=1, keepdims=True)
    tag_all = jnp.broadcast_to(tag_col, own_tag.shape)
    own_tag[...] = tag_all.astype(jnp.int32)
    levels_ref[...] = jnp.transpose(tag_all)[0:8, :].astype(jnp.int32) - 1
    row = iota((edge * cap, rows), 0)
    for i in range(owners):
        hit = jnp.where(row == targets[i], 1.0, 0.0).astype(jnp.bfloat16)
        unpack[:, i * rows : i * rows + rows] = hit

    def near_copy(up):
        to = node + 1 if up else node - 1
        index = 0 if up else 1
        return pltpu.make_async_remote_copy(
            src_ref=own_tag, dst_ref=near_tag.at[index],
            send_sem=near_send.at[index], recv_sem=near_recv.at[index],
            device_id={"node": to}, device_id_type=MESH,
        )

    def ghost_copy(q, up):
        to = node + 1 if up else node - 1
        index = 0 if up else 1
        return pltpu.make_async_remote_copy(
            src_ref=gsend.at[index, q], dst_ref=grecv.at[index, q],
            send_sem=gh_send.at[index, q], recv_sem=gh_recv.at[index, q],
            device_id={"node": to}, device_id_type=MESH,
        )

    @pl.when(has_high)
    def _():
        near_copy(True).start()

    @pl.when(has_low)
    def _():
        near_copy(False).start()

    @pl.when(has_low)
    def _():
        near_copy(True).wait_recv()

    @pl.when(has_high)
    def _():
        near_copy(False).wait_recv()

    def front(q):
        at = split_low(q, 2)
        for r in range(1, owners):
            block_arrival(q, r).wait_recv()
        sources = inc[q].reshape(owners * rows, plane)

        def arrange(low, high):
            part = jnp.dot(
                unpack[low * cap : high * cap, :], sources, preferred_element_type=jnp.float32
            )
            ext[at, GHOST + low : GHOST + high] = part.reshape(high - low, cap, plane)

        arrange(0, 2 * GHOST)
        arrange(edge - 2 * GHOST, edge)
        for up in (True, False):
            index = 0 if up else 1
            gap = own_tag[...] - near_tag[1 - index]
            for half in range(plane // 128):
                lanes = slice(half * 128, half * 128 + 128)
                near = [
                    ext[at, GHOST + (edge - 1 - k if up else k), :, lanes]
                    for k in range(2 * GHOST)
                ]
                for k in range(GHOST):
                    finer = 0.5 * (near[2 * k] + near[2 * k + 1])
                    ghost = jnp.where(gap > 0, finer, jnp.where(gap < 0, near[k // 2 if k else 0], near[k]))
                    gsend[index, q, GHOST - 1 - k if up else k, :, lanes] = ghost.astype(jnp.bfloat16)
        arrange(2 * GHOST, edge - 2 * GHOST)

    def send(q):
        @pl.when(has_high)
        def _():
            ghost_copy(q, True).start()

        @pl.when(has_low)
        def _():
            ghost_copy(q, False).start()

    lane_tiles = plane // 128
    tiles = (cap // 8) * lane_tiles

    def tiles_of(q):
        at = split_low(q, 2)
        speed, threshold = speed_ref[q], threshold_ref[q]
        neg = jnp.full((8, 128), speed, jnp.float32) < 0.0
        size = jnp.full((8, 128), jnp.abs(speed), jnp.float32)
        bound = jnp.full((8, 128), threshold, jnp.float32)

        def one(tile, carry):
            top = pl.multiple_of((tile // lane_tiles) * 8, 8)
            lanes = pl.ds(pl.multiple_of((tile % lane_tiles) * 128, 128), 128)
            cells = [ext[at, i, pl.ds(top, 8), lanes] for i in range(edge + 2 * GHOST)]
            result = advance_tile(cells, neg, size, bound)
            occupied = own_tag[pl.ds(top, 8), :] > 0
            for c in range(edge):
                value = jnp.where(occupied, result[c], 0.0)
                wide[tile % lane_tiles, pl.ds(top * edge + c, 8, stride=edge), :] = value
            return carry

        lax.fori_loop(0, tiles, one, 0)

    def back(q):
        at = split_low(q, 2)

        @pl.when(has_low)
        def _():
            ghost_copy(q, True).wait_recv()

        @pl.when(has_high)
        def _():
            ghost_copy(q, False).wait_recv()

        ext[at, 0:GHOST] = grecv[0, q].astype(jnp.float32)
        ext[at, GHOST + edge :] = grecv[1, q].astype(jnp.float32)
        tiles_of(q)
        for half in range(lane_tiles):
            out_ref[:, q, :, half * 128 : half * 128 + 128] = (
                wide[half].astype(jnp.bfloat16).reshape(cap, edge, 128)
            )

    front(jnp.int32(0))
    send(jnp.int32(0))

    @pl.loop(1, quant)
    def _(q):
        front(q)
        send(q)
        back(q - 1)

    last = jnp.int32(quant - 1)
    back(last)

    for r in range(1, owners):
        tag_copy(r).wait_send()

    @pl.when(has_high)
    def _():
        near_copy(True).wait_send()

    @pl.when(has_low)
    def _():
        near_copy(False).wait_send()

    @pl.loop(0, quant)
    def _(q):
        for r in range(1, owners):
            block_copy(q, r).wait_send()

        @pl.when(has_high)
        def _():
            ghost_copy(q, True).wait_send()

        @pl.when(has_low)
        def _():
            ghost_copy(q, False).wait_send()


def body(blocks, levels, destinations, speeds, thresholds):
    owners, groups = lax.axis_size("dev"), lax.axis_size("node")
    _, _, slots, quant, edge, plane = blocks.shape
    pair = max(1, (2 * slots + owners - 1) // owners)
    rows = edge * pair
    cells = edge + 2 * GHOST
    dma = pltpu.SemaphoreType.DMA
    updated, new_levels = pl.pallas_call(
        functools.partial(step_kernel, owners, groups, pair),
        in_specs=[pl.BlockSpec(memory_space=pltpu.HBM)] * 5,
        out_specs=[pl.BlockSpec(memory_space=pltpu.VMEM)] * 2,
        out_shape=[
            jax.ShapeDtypeStruct((NEW_CAP, quant, edge, plane), jnp.bfloat16),
            jax.ShapeDtypeStruct((8, NEW_CAP), jnp.int32),
        ],
        scratch_shapes=[
            pltpu.SMEM((slots,), jnp.int32), pltpu.SMEM((slots,), jnp.int32),
            pltpu.SMEM((quant,), jnp.float32), pltpu.SMEM((quant,), jnp.float32),
            pltpu.VMEM((quant, slots, edge, plane), jnp.bfloat16),
            pltpu.VMEM((owners * rows, slots * edge), jnp.bfloat16),
            pltpu.VMEM((quant, owners, rows, plane), jnp.bfloat16),
            pltpu.VMEM((owners, 8, rows), jnp.int32),
            pltpu.VMEM((quant, owners, rows, plane), jnp.bfloat16),
            pltpu.VMEM((owners, 8, rows), jnp.int32),
            pltpu.VMEM((edge * NEW_CAP, owners * rows), jnp.bfloat16),
            pltpu.VMEM((2, cells, NEW_CAP, plane), jnp.float32),
            pltpu.VMEM((2, quant, GHOST, NEW_CAP, plane), jnp.bfloat16),
            pltpu.VMEM((2, quant, GHOST, NEW_CAP, plane), jnp.bfloat16),
            pltpu.VMEM((NEW_CAP, 128), jnp.int32),
            pltpu.VMEM((2, NEW_CAP, 128), jnp.int32),
            pltpu.VMEM((plane // 128, NEW_CAP * edge, 128), jnp.float32),
            dma((4,)), dma((quant,)), dma((owners,)), dma((owners,)),
            dma((quant, owners)), dma((quant, owners)),
            dma((2,)), dma((2,)), dma((2, quant)), dma((2, quant)),
        ],
        compiler_params=pltpu.CompilerParams(
            collective_id=0, has_side_effects=True, vmem_limit_bytes=48 * 1024 * 1024
        ),
        name="step",
    )(
        *(
            pltpu.with_memory_space_constraint(x, pltpu.HBM)
            for x in (destinations[0, 0], levels[0, 0], blocks[0, 0], speeds, thresholds)
        )
    )
    return (
        updated.reshape(1, 1, NEW_CAP, quant, edge, plane),
        new_levels[0].reshape(1, 1, NEW_CAP),
    )


def solution(mesh):
    return jax.shard_map(
        body,
        mesh=mesh,
        in_specs=(
            P("node", "dev", None, None, None, None),
            P("node", "dev", None),
            P("node", "dev", None),
            P(),
            P(),
        ),
        out_specs=(P("node", "dev", None, None, None, None), P("node", "dev", None)),
        check_vma=False,
    )
```

```python
import functools

import jax
import jax.numpy as jnp
from jax import lax
from jax.experimental import pallas as pl
from jax.experimental.pallas import tpu as pltpu
from jax.sharding import PartitionSpec as P

NEW_CAP = 32
GHOST = 3
COURANT = 0.4
WENO_EPS = 1e-06
MESH = pl.DeviceIdType.MESH


def iota(shape, dim):
    return lax.broadcasted_iota(jnp.int32, shape, dim)


def split_low(values, size):
    return values & (size - 1)


def partner(me, r):
    result, bit = 0, 1
    while bit <= r:
        own = me // bit % 2
        result = result + bit * ((1 - own) if r & bit else own)
        bit *= 2
    return result + me // bit * bit


def split_high(values, size):
    return values >> (size.bit_length() - 1)


def plan_sends(owners, pair, edge, dest_ref, level_ref, place_ref, tags_ref):
    slots = dest_ref.shape[0]
    rows = edge * pair
    lanes = slots * edge
    dest = [dest_ref[s] for s in range(slots)]
    within = []
    for s in range(slots):
        count = jnp.int32(0)
        for before in range(s):
            count = count + jnp.where(dest[before] == dest[s], 1, 0)
        within.append(count)
    lane = iota((1, lanes), 1)
    slot_of = split_high(lane, edge)
    target = jnp.zeros((1, lanes), jnp.int32)
    for s in range(slots):
        target = jnp.where(slot_of == s, dest[s] * rows + within[s], target)
    target = target + split_low(lane, edge) * pair
    hit = iota((owners * rows, lanes), 0) == target
    place_ref[...] = jnp.where(hit, 1.0, 0.0).astype(jnp.bfloat16)
    owner = iota(tags_ref.shape, 0)
    slot = split_low(iota(tags_ref.shape, 2), pair)
    tags = jnp.zeros(tags_ref.shape, jnp.int32)
    for s in range(slots):
        here = (owner == dest[s]) & (slot == within[s])
        tags = jnp.where(here, level_ref[s] + 1, tags)
    tags_ref[...] = tags


def advance_tile(cells, neg, speed, threshold):
    total = len(cells)
    edge = total - 2 * GHOST
    m = [jnp.where(neg, cells[total - 1 - i], cells[i]) for i in range(total)]
    d = [m[i + 1] - m[i] for i in range(total - 2)]
    d2 = [x + x for x in d]
    s = [None] + [d[i] - d[i - 1] for i in range(1, total - 2)]
    base = [None] + [(13.0 / 3.0) * (x * x) + 4.0 * WENO_EPS for x in s[1:]]
    shift = []
    for f in range(edge + 1):
        low, high = d[f + 1], d[f + 2]
        t0 = s[f + 1] + d2[f + 1]
        t1 = low + high
        t2 = d2[f + 2] - s[f + 3]
        b0 = base[f + 1] + t0 * t0
        b1 = base[f + 2] + t1 * t1
        b2 = base[f + 3] + t2 * t2
        w0, w1, w2 = b1 * b2, b0 * b2, b0 * b1
        w0, w1, w2 = w0 * w0, 6.0 * (w1 * w1), 3.0 * (w2 * w2)
        p0 = t0 + t0 - low
        p1 = low + d2[f + 2]
        p2 = t2 + high
        shift.append((w0 * p0 + w1 * p1 + w2 * p2) / (w0 + w1 + w2))
    full = COURANT * speed
    sixth = full / 6.0
    moved = [
        m[c + GHOST] - (full * d[c + 2] + sixth * (shift[c + 1] - shift[c]))
        for c in range(edge)
    ]
    adv = [jnp.where(neg, moved[edge - 1 - c], moved[c]) for c in range(edge)]
    result = list(adv)
    for k in range(1, edge, 2):
        guess = 0.5 * (adv[k - 1] + adv[k + 1]) if k + 1 < edge else adv[k - 1]
        detail = adv[k] - guess
        result[k] = guess + detail - jnp.clip(detail, -threshold, threshold)
    return result


def step_kernel(
    owners, groups, pair,
    dest_hbm, level_hbm, block_hbm, speed_hbm, threshold_hbm,
    out_ref, levels_ref,
    dest_ref, level_ref, speed_ref, threshold_ref,
    payload, place, packed_ref, tags_ref,
    inc, tin, unpack, ext, gsend, grecv, own_tag, near_tag, wide,
    load_sem, block_sem, tag_send, tag_recv, blk_send, blk_recv,
    near_send, near_recv, gh_send, gh_recv,
):
    node = lax.axis_index("node")
    me = lax.axis_index("dev")
    slots, quant, edge, plane = block_hbm.shape
    rows = edge * pair
    cap = own_tag.shape[0]
    has_low = node > 0
    has_high = node < groups - 1

    small = [
        pltpu.make_async_copy(source, target, load_sem.at[n])
        for n, (source, target) in enumerate(
            (
                (dest_hbm, dest_ref), (level_hbm, level_ref),
                (speed_hbm, speed_ref), (threshold_hbm, threshold_ref),
            )
        )
    ]
    for copy in small:
        copy.start()

    def load(q):
        return pltpu.make_async_copy(block_hbm.at[:, q], payload.at[q], block_sem.at[q])

    @pl.loop(0, quant)
    def _(q):
        load(q).start()

    barrier = pltpu.get_barrier_semaphore()
    for r in range(1, owners):
        pl.semaphore_signal(
            barrier, inc=1, device_id={"dev": partner(me, r)}, device_id_type=MESH
        )

    @pl.when(has_low)
    def _():
        pl.semaphore_signal(barrier, inc=1, device_id={"node": node - 1}, device_id_type=MESH)

    @pl.when(has_high)
    def _():
        pl.semaphore_signal(barrier, inc=1, device_id={"node": node + 1}, device_id_type=MESH)

    for copy in small:
        copy.wait()
    plan_sends(owners, pair, edge, dest_ref, level_ref, place, tags_ref)
    def tag_copy(r):
        return pltpu.make_async_remote_copy(
            src_ref=tags_ref.at[partner(me, r)], dst_ref=tin.at[me],
            send_sem=tag_send.at[r], recv_sem=tag_recv.at[r],
            device_id={"dev": partner(me, r)}, device_id_type=MESH,
        )

    def tag_arrival(r):
        return pltpu.make_async_remote_copy(
            src_ref=tags_ref.at[me], dst_ref=tin.at[partner(me, r)],
            send_sem=tag_send.at[r], recv_sem=tag_recv.at[r],
            device_id={"dev": partner(me, r)}, device_id_type=MESH,
        )

    def block_copy(q, r):
        to = partner(me, r)
        return pltpu.make_async_remote_copy(
            src_ref=packed_ref.at[q, to], dst_ref=inc.at[q, me],
            send_sem=blk_send.at[q, r], recv_sem=blk_recv.at[q, r],
            device_id={"dev": to}, device_id_type=MESH,
        )

    def block_arrival(q, r):
        return pltpu.make_async_remote_copy(
            src_ref=packed_ref.at[q, me], dst_ref=inc.at[q, partner(me, r)],
            send_sem=blk_send.at[q, r], recv_sem=blk_recv.at[q, r],
            device_id={"dev": partner(me, r)}, device_id_type=MESH,
        )

    def pack(q):
        load(q).wait()
        flat = payload[q].reshape(slots * edge, plane)
        rows_of = jnp.dot(place[...], flat, preferred_element_type=jnp.float32)
        packed_ref[q] = rows_of.astype(jnp.bfloat16).reshape(owners, rows, plane)

    def launch(q):
        for r in range(1, owners):
            block_copy(q, r).start()

    def keep(q):
        inc[q, me] = packed_ref[q, me]

    pack(jnp.int32(0))
    nears = (node + groups - 1) // groups + (2 * groups - 2 - node) // groups
    pl.semaphore_wait(barrier, owners - 1 + nears)
    for r in range(1, owners):
        tag_copy(r).start()
    launch(jnp.int32(0))
    tin[me] = tags_ref[me]
    keep(0)
    pack(jnp.int32(1))

    @pl.loop(2, quant)
    def _(q):
        pack(q)
        launch(q - 1)
        keep(q - 1)

    launch(jnp.int32(quant - 1))
    keep(quant - 1)

    @pl.when(node == 0)
    def _():
        grecv[0] = jnp.zeros(grecv.shape[1:], grecv.dtype)
        near_tag[0] = jnp.zeros(near_tag.shape[1:], near_tag.dtype)

    @pl.when(node == groups - 1)
    def _():
        grecv[1] = jnp.zeros(grecv.shape[1:], grecv.dtype)
        near_tag[1] = jnp.zeros(near_tag.shape[1:], near_tag.dtype)

    for r in range(1, owners):
        tag_arrival(r).wait_recv()

    lane = iota((1, rows), 1)
    slot, cell = split_low(lane, pair), split_high(lane, pair)
    first = jnp.zeros((1, 1), jnp.float32)
    tag_sum = jnp.zeros((cap, rows), jnp.float32)
    row_p = iota((cap, rows), 0)
    targets = []
    for i in range(owners):
        tag = tin[i, 0:1, :]
        present = tag > 0
        position = first.astype(jnp.int32) + slot
        targets.append(jnp.where(present, cell * cap + position, -1))
        here = (row_p == jnp.where(present & (cell == 0), position, -1))
        tag_sum = tag_sum + jnp.where(here, tag.astype(jnp.float32), 0.0)
        count = jnp.sum(jnp.where(present, 1.0, 0.0), axis=1, keepdims=True)
        first = first + count * (1.0 / edge)
    tag_col = jnp.sum(tag_sum, axis=1, keepdims=True)
    tag_all = jnp.broadcast_to(tag_col, own_tag.shape)
    own_tag[...] = tag_all.astype(jnp.int32)
    levels_ref[...] = jnp.transpose(tag_all)[0:8, :].astype(jnp.int32) - 1
    row = iota((edge * cap, rows), 0)
    for i in range(owners):
        hit = jnp.where(row == targets[i], 1.0, 0.0).astype(jnp.bfloat16)
        unpack[:, i * rows : i * rows + rows] = hit

    def near_copy(up):
        to = node + 1 if up else node - 1
        index = 0 if up else 1
        return pltpu.make_async_remote_copy(
            src_ref=own_tag, dst_ref=near_tag.at[index],
            send_sem=near_send.at[index], recv_sem=near_recv.at[index],
            device_id={"node": to}, device_id_type=MESH,
        )

    def ghost_copy(q, up):
        to = node + 1 if up else node - 1
        index = 0 if up else 1
        return pltpu.make_async_remote_copy(
            src_ref=gsend.at[index, q], dst_ref=grecv.at[index, q],
            send_sem=gh_send.at[index, q], recv_sem=gh_recv.at[index, q],
            device_id={"node": to}, device_id_type=MESH,
        )

    @pl.when(has_high)
    def _():
        near_copy(True).start()

    @pl.when(has_low)
    def _():
        near_copy(False).start()

    @pl.when(has_low)
    def _():
        near_copy(True).wait_recv()

    @pl.when(has_high)
    def _():
        near_copy(False).wait_recv()

    def front(q):
        at = split_low(q, 2)
        for r in range(1, owners):
            block_arrival(q, r).wait_recv()
        sources = inc[q].reshape(owners * rows, plane)

        def arrange(low, high):
            part = jnp.dot(
                unpack[low * cap : high * cap, :], sources, preferred_element_type=jnp.float32
            )
            ext[at, GHOST + low : GHOST + high] = part.reshape(high - low, cap, plane)

        arrange(0, 2 * GHOST)
        arrange(edge - 2 * GHOST, edge)
        for up in (True, False):
            index = 0 if up else 1
            gap = own_tag[...] - near_tag[1 - index]
            for half in range(plane // 128):
                lanes = slice(half * 128, half * 128 + 128)
                near = [
                    ext[at, GHOST + (edge - 1 - k if up else k), :, lanes]
                    for k in range(2 * GHOST)
                ]
                for k in range(GHOST):
                    finer = 0.5 * (near[2 * k] + near[2 * k + 1])
                    ghost = jnp.where(gap > 0, finer, jnp.where(gap < 0, near[k // 2 if k else 0], near[k]))
                    gsend[index, q, GHOST - 1 - k if up else k, :, lanes] = ghost.astype(jnp.bfloat16)
        arrange(2 * GHOST, edge - 2 * GHOST)

    def send(q):
        @pl.when(has_high)
        def _():
            ghost_copy(q, True).start()

        @pl.when(has_low)
        def _():
            ghost_copy(q, False).start()

    lane_tiles = plane // 128
    tiles = (cap // 8) * lane_tiles

    def tiles_of(q):
        at = split_low(q, 2)
        speed, threshold = speed_ref[q], threshold_ref[q]
        neg = jnp.full((8, 128), speed, jnp.float32) < 0.0
        size = jnp.full((8, 128), jnp.abs(speed), jnp.float32)
        bound = jnp.full((8, 128), threshold, jnp.float32)

        def one(tile, carry):
            top = pl.multiple_of((tile // lane_tiles) * 8, 8)
            lanes = pl.ds(pl.multiple_of((tile % lane_tiles) * 128, 128), 128)
            cells = [ext[at, i, pl.ds(top, 8), lanes] for i in range(edge + 2 * GHOST)]
            result = advance_tile(cells, neg, size, bound)
            occupied = own_tag[pl.ds(top, 8), :] > 0
            for c in range(edge):
                value = jnp.where(occupied, result[c], 0.0)
                wide[tile % lane_tiles, pl.ds(top * edge + c, 8, stride=edge), :] = value
            return carry

        lax.fori_loop(0, tiles, one, 0)

    def back(q):
        at = split_low(q, 2)

        @pl.when(has_low)
        def _():
            ghost_copy(q, True).wait_recv()

        @pl.when(has_high)
        def _():
            ghost_copy(q, False).wait_recv()

        ext[at, 0:GHOST] = grecv[0, q].astype(jnp.float32)
        ext[at, GHOST + edge :] = grecv[1, q].astype(jnp.float32)
        tiles_of(q)
        for half in range(lane_tiles):
            out_ref[:, q, :, half * 128 : half * 128 + 128] = (
                wide[half].astype(jnp.bfloat16).reshape(cap, edge, 128)
            )

    front(jnp.int32(0))
    send(jnp.int32(0))

    @pl.loop(1, quant)
    def _(q):
        front(q)
        send(q)
        back(q - 1)

    last = jnp.int32(quant - 1)
    back(last)

    for r in range(1, owners):
        tag_copy(r).wait_send()

    @pl.when(has_high)
    def _():
        near_copy(True).wait_send()

    @pl.when(has_low)
    def _():
        near_copy(False).wait_send()

    @pl.loop(0, quant)
    def _(q):
        for r in range(1, owners):
            block_copy(q, r).wait_send()

        @pl.when(has_high)
        def _():
            ghost_copy(q, True).wait_send()

        @pl.when(has_low)
        def _():
            ghost_copy(q, False).wait_send()


def body(blocks, levels, destinations, speeds, thresholds):
    owners, groups = lax.axis_size("dev"), lax.axis_size("node")
    _, _, slots, quant, edge, plane = blocks.shape
    pair = max(1, (2 * slots + owners - 1) // owners)
    rows = edge * pair
    cells = edge + 2 * GHOST
    dma = pltpu.SemaphoreType.DMA
    updated, new_levels = pl.pallas_call(
        functools.partial(step_kernel, owners, groups, pair),
        in_specs=[pl.BlockSpec(memory_space=pltpu.HBM)] * 5,
        out_specs=[pl.BlockSpec(memory_space=pltpu.VMEM)] * 2,
        out_shape=[
            jax.ShapeDtypeStruct((NEW_CAP, quant, edge, plane), jnp.bfloat16),
            jax.ShapeDtypeStruct((8, NEW_CAP), jnp.int32),
        ],
        scratch_shapes=[
            pltpu.SMEM((slots,), jnp.int32), pltpu.SMEM((slots,), jnp.int32),
            pltpu.SMEM((quant,), jnp.float32), pltpu.SMEM((quant,), jnp.float32),
            pltpu.VMEM((quant, slots, edge, plane), jnp.bfloat16),
            pltpu.VMEM((owners * rows, slots * edge), jnp.bfloat16),
            pltpu.VMEM((quant, owners, rows, plane), jnp.bfloat16),
            pltpu.VMEM((owners, 8, rows), jnp.int32),
            pltpu.VMEM((quant, owners, rows, plane), jnp.bfloat16),
            pltpu.VMEM((owners, 8, rows), jnp.int32),
            pltpu.VMEM((edge * NEW_CAP, owners * rows), jnp.bfloat16),
            pltpu.VMEM((2, cells, NEW_CAP, plane), jnp.float32),
            pltpu.VMEM((2, quant, GHOST, NEW_CAP, plane), jnp.bfloat16),
            pltpu.VMEM((2, quant, GHOST, NEW_CAP, plane), jnp.bfloat16),
            pltpu.VMEM((NEW_CAP, 128), jnp.int32),
            pltpu.VMEM((2, NEW_CAP, 128), jnp.int32),
            pltpu.VMEM((plane // 128, NEW_CAP * edge, 128), jnp.float32),
            dma((4,)), dma((quant,)), dma((owners,)), dma((owners,)),
            dma((quant, owners)), dma((quant, owners)),
            dma((2,)), dma((2,)), dma((2, quant)), dma((2, quant)),
        ],
        compiler_params=pltpu.CompilerParams(
            collective_id=0, has_side_effects=True, vmem_limit_bytes=48 * 1024 * 1024
        ),
        name="step",
    )(
        *(
            pltpu.with_memory_space_constraint(x, pltpu.HBM)
            for x in (destinations[0, 0], levels[0, 0], blocks[0, 0], speeds, thresholds)
        )
    )
    return (
        updated.reshape(1, 1, NEW_CAP, quant, edge, plane),
        new_levels[0].reshape(1, 1, NEW_CAP),
    )


def solution(mesh):
    return jax.shard_map(
        body,
        mesh=mesh,
        in_specs=(
            P("node", "dev", None, None, None, None),
            P("node", "dev", None),
            P("node", "dev", None),
            P(),
            P(),
        ),
        out_specs=(P("node", "dev", None, None, None, None), P("node", "dev", None)),
        check_vma=False,
    )
```
